32 devices in a mesh: seq: 8 (over y, x, core), mp: 4 (over z).
Axes of the slice: x: 2, y: 2, z: 4, core: 2. Of those that a mesh axis runs over, the one named last changes fastest.
Arguments:
- tokens: bfloat16 [1024, 4096], P('seq', 'mp'), may hold values from -10 to 10
- norm_gain: float32 [4096], replicated, may hold values from 0.1 to 1.9
- w_cand: bfloat16 [4096, 4096], P('seq', 'mp'), may hold values from -0.125 to 0.125
- w_gate: bfloat16 [4096, 4096], P('seq', 'mp'), may hold values from -0.046875 to 0.046875
- rec_gate: float32 [4096], P('mp'), may hold values from -0.75 to 0.75
- rec_cand: float32 [4096], P('mp'), may hold values from -0.6 to 0.6
- bias_gate: float32 [4096], P('mp')
- w_out: bfloat16 [4096, 4096], P('mp'), may hold values from -0.09375 to 0.09375
Outputs:
- output: bfloat16 [1024, 4096], P('seq', 'mp')
The draws below stay inside these ranges and needn't reach their ends.
All inputs are finite; a program needn't handle non-finite values.
Results may differ from the reference program's by a relative error of at most 0.0048.
Values may be sent and summed in bfloat16 or wider, within the bound.
A program may use at most 64 MiB of HBM per device.

```python
import jax
import jax.numpy as jnp
from jax import lax

D = 4096
NEWTON = 3
LENGTH = 1024


def draw_bias_gate(key, part):
    first = jax.random.fold_in(key, 0)
    lowest = jnp.log(0.3 / LENGTH)
    highest = jnp.log(0.03)
    lograte = jax.random.uniform(first, (D,), jnp.float32, lowest, highest)
    rate = jnp.exp(lograte)
    return jnp.log((1.0 - rate) / rate)


def draw_tokens(key, part):
    first, second = jax.random.split(jax.random.fold_in(key, 71), 2)
    segment = (jnp.arange(LENGTH) * 8 // LENGTH).astype(jnp.int32)
    topics = 2.0 * jnp.clip(jax.random.normal(first, (8, D), jnp.float32), -2.5, 2.5)
    noise = jnp.clip(jax.random.normal(second, (LENGTH, D), jnp.float32), -3.0, 3.0)
    values = jnp.take(topics, segment, axis=0) + noise
    return jnp.clip(values, -10.0, 10.0).astype(jnp.bfloat16)


def levels(own_key, shape, cuts, low, largest):
    def one(position, blocks):
        draws = jax.random.uniform(jax.random.fold_in(jax.random.fold_in(own_key, 6), position), (blocks,), jnp.float32, low / len(cuts), largest / len(cuts))
        return jnp.repeat(jnp.exp(draws), shape[position] // blocks).reshape((-1,) + (1,) * (len(shape) - position - 1))

    loudness = one(*cuts[0])
    for cut in cuts[1:]:
        loudness = loudness * one(*cut)
    return loudness


def scatter_about(key, dims, deviation, limit, pieces=(), kind=jnp.bfloat16):
    values = jax.random.normal(key, dims, jnp.float32) * deviation
    if len(pieces) > 0:
        values = levels(key, dims, pieces, -0.22, 0.18) * values
    return jnp.clip(values, min=-limit, max=limit).astype(kind)


def setup_inputs(seed: int = 0) -> dict:
    streams_of = jax.random.split(jax.random.key(seed), 9)
    return {
        "tokens": draw_tokens(jax.random.fold_in(streams_of[8], 71), 0),
        "norm_gain": jnp.clip(1.0 + 0.18 * jax.random.normal(streams_of[1], (D,), jnp.float32), 0.1, 1.9),
        "w_cand": scatter_about(streams_of[2], (D, D), (D // 2) ** -0.5, 0.125, ((0, 8), (1, 4))),
        "w_gate": scatter_about(streams_of[3], (D, D), (4 * D) ** -0.5, 0.046875, ((0, 8), (1, 4))),
        "rec_gate": jnp.clip(jax.random.uniform(streams_of[4], (D,), jnp.float32, -0.75, 0.75) * levels(streams_of[4], (D,), ((0, 4),), -0.4, 0.0), -0.75, 0.75),
        "rec_cand": jnp.clip(jax.random.uniform(streams_of[5], (D,), jnp.float32, -0.6, 0.6) * levels(streams_of[5], (D,), ((0, 4),), -0.4, 0.0), -0.6, 0.6),
        "bias_gate": draw_bias_gate(jax.random.fold_in(streams_of[8], 71), 0),
        "w_out": scatter_about(streams_of[7], (D, D), D ** -0.5, 0.09375, ((0, 4),)),
    }


def compose(earlier, later):
    return (later[0] * earlier[0], later[0] * earlier[1] + later[1])

def cell(previous, cand_pre, gate_pre, rec_gate, rec_cand, bias_gate):
    gate = jax.nn.sigmoid(gate_pre + rec_gate * previous + bias_gate)
    cand = jnp.tanh(cand_pre + rec_cand * previous)
    value = gate * previous + (1.0 - gate) * cand
    slope = gate + gate * (1.0 - gate) * rec_gate * (previous - cand) + (1.0 - gate) * (1.0 - cand * cand) * rec_cand
    return (value, slope)

def reference(tokens, norm_gain, w_cand, w_gate, rec_gate, rec_cand, bias_gate, w_out):
    wide = tokens.astype(jnp.float32)
    factor = lax.rsqrt(lax.optimization_barrier(jnp.mean(wide * wide, axis=1, keepdims=True)) + 1e-05)
    normed = (wide * factor * norm_gain).astype(jnp.bfloat16)
    cand_pre = jnp.dot(normed, w_cand, preferred_element_type=jnp.float32)
    gate_pre = jnp.dot(normed, w_gate, preferred_element_type=jnp.float32)
    state = jnp.zeros(cand_pre.shape, jnp.float32)
    for newton_step in range(NEWTON):
        previous = jnp.concatenate([jnp.zeros((1, state.shape[1]), jnp.float32), state[:-1]], axis=0)
        value, slope = cell(previous, cand_pre, gate_pre, rec_gate, rec_cand, bias_gate)
        offset = value - slope * previous
        sweep = lax.associative_scan(compose, (slope, offset), axis=0)
        state = sweep[1]
    state_b = state.astype(jnp.bfloat16)
    return jnp.dot(state_b, w_out, preferred_element_type=jnp.float32).astype(jnp.bfloat16)
```

```python
import functools

import jax
import jax.numpy as jnp
from jax import lax
from jax.experimental import pallas as pl
from jax.experimental.pallas import tpu as pltpu
from jax.sharding import PartitionSpec as P

NEWTON = 3


def prefix(value, axis, join, neutral):
    count, mine = (lax.axis_size(axis), lax.axis_index(axis))
    pieces = jax.tree.map(lambda part: lax.all_gather(part, axis), value)
    subtotal = jax.tree.map(
        lambda part, zero: jnp.full_like(part, 0) + jnp.asarray(zero, part.dtype), value, neutral
    )

    def lap(position, subtotal):
        longer = join(subtotal, jax.tree.map(lambda part: part[position], pieces))
        return jax.tree.map(lambda new, old: jnp.where(position < mine, new, old), longer, subtotal)

    return lax.fori_loop(0, count - 1, lap, subtotal)


def compose(earlier, later):
    return (later[0] * earlier[0], later[0] * earlier[1] + later[1])


def cell(previous, cand_pre, gate_pre, rec_gate, rec_cand, bias_gate):
    gate = jax.nn.sigmoid(gate_pre + rec_gate * previous + bias_gate)
    cand = jnp.tanh(cand_pre + rec_cand * previous)
    value = gate * previous + (1.0 - gate) * cand
    slope = (
        gate
        + gate * (1.0 - gate) * rec_gate * (previous - cand)
        + (1.0 - gate) * (1.0 - cand * cand) * rec_cand
    )
    return (value, slope)


def per_device(tokens, norm_gain, w_cand, w_gate, rec_gate, rec_cand, bias_gate, w_out):
    tok_rows = tokens.shape[0]
    channels = w_cand.shape[1]
    whole = lax.all_gather(tokens, "mp", axis=1, tiled=True)
    wide = whole.astype(jnp.float32)
    factor = lax.rsqrt(jnp.mean(wide * wide, axis=1, keepdims=True) + 1e-05)
    normed = (wide * factor * norm_gain).astype(jnp.bfloat16)
    cand_pre = jnp.dot(
        normed,
        lax.all_gather(w_cand, "seq", axis=0, tiled=True),
        preferred_element_type=jnp.float32,
    )
    gate_pre = jnp.dot(
        normed,
        lax.all_gather(w_gate, "seq", axis=0, tiled=True),
        preferred_element_type=jnp.float32,
    )
    state = jnp.zeros((tok_rows, channels), jnp.float32)
    carried = jnp.zeros((channels,), jnp.float32)
    ones_row = jnp.ones((channels,), jnp.float32)
    for newton_step in range(NEWTON):
        previous = jnp.concatenate([carried[None, :], state[:-1]], axis=0)
        value, slope = cell(previous, cand_pre, gate_pre, rec_gate, rec_cand, bias_gate)
        offset = value - slope * previous
        sweep_a, sweep_b = lax.associative_scan(compose, (slope, offset), axis=0)
        entering = prefix((sweep_a[-1], sweep_b[-1]), "seq", compose, (ones_row, carried * 0.0))
        carried = entering[1]
        state = sweep_a * carried + sweep_b
    state_b = state.astype(jnp.bfloat16)
    partial_sums = jnp.dot(state_b, w_out, preferred_element_type=jnp.float32)
    summed = lax.psum_scatter(partial_sums, "mp", scatter_dimension=1, tiled=True)
    return summed.astype(jnp.bfloat16)


CORES = 2
SUBLANES = 8
LANES = 128
MESH = pl.DeviceIdType.MESH


def fused_kernel(
    n_seq,
    n_mp,
    tok_ref,
    gain_ref,
    wc_hbm,
    wg_hbm,
    rg_ref,
    rc_ref,
    bg_ref,
    wo_hbm,
    out_ref,
    raw,
    nsend,
    xk,
    wk,
    wo,
    own,
    psend,
    precv,
    cand_n,
    gate_n,
    sweep_a,
    sweep_b,
    carry,
    ssend,
    sall,
    pout,
    osend,
    orecv,
    w_loc,
    w_snd,
    w_rcv,
    wo_sem,
    z_snd,
    z_rcv,
    k_snd,
    k_rcv,
    f_snd,
    p_snd,
    p_rcv,
    s_snd,
    s_rcv,
    o_snd,
    o_rcv,
):
    s, m = (lax.axis_index("seq"), lax.axis_index("mp"))
    n_chip = n_seq // CORES
    c, r = (s // CORES, s % CORES)
    mate = c * CORES + (1 - r)
    rows = tok_ref.shape[0]
    tokens = rows * n_seq
    k_own = wc_hbm.shape[0]
    width = raw.shape[2]
    q = r * n_chip + c

    def remote(src, dst, snd, rcv, **where):
        return pltpu.make_async_remote_copy(
            src_ref=src, dst_ref=dst, send_sem=snd, recv_sem=rcv, device_id=where, device_id_type=MESH
        )

    def barrier():
        sem = pltpu.get_barrier_semaphore()
        for o in range(1, n_seq):
            pl.semaphore_signal(sem, inc=1, device_id={"seq": (s + o) % n_seq}, device_id_type=MESH)
        for o in range(1, n_mp):
            pl.semaphore_signal(sem, inc=1, device_id={"mp": (m + o) % n_mp}, device_id_type=MESH)
        pl.semaphore_wait(sem, n_seq + n_mp - 2)

    def w_piece(hbm, core, chip):
        return hbm.at[:, pl.ds(pl.multiple_of((core * n_chip + chip) * LANES, LANES), LANES)]

    def w_place(i, chip, core):
        return wk.at[chip, pl.ds(pl.multiple_of(core * k_own, k_own), k_own), pl.ds(i * LANES, LANES)]

    local = [
        pltpu.make_async_copy(w_piece(hbm, r, chip), w_place(i, chip, r), w_loc.at[i, chip])
        for chip in range(n_chip)
        for i, hbm in enumerate((wc_hbm, wg_hbm))
    ]
    wo_copy = pltpu.make_async_copy(wo_hbm, wo, wo_sem)
    for copy in local:
        copy.start()
    barrier()

    def right_copy(src, b, k):
        return remote(src, raw.at[b], z_snd.at[0, k], z_rcv.at[b], mp=(m + 1) % n_mp)

    def left_copy(src, b, k):
        return remote(src, raw.at[b], z_snd.at[1, k], z_rcv.at[b], mp=(m + n_mp - 1) % n_mp)

    @pl.when(m < n_mp - 1)
    def _():
        right_copy(tok_ref, m, 0).start()

    @pl.when(m > 0)
    def _():
        left_copy(tok_ref, m, 0).start()

    w_out_copies = [
        remote(w_piece(hbm, 1 - r, chip), w_place(i, chip, r), w_snd.at[i, chip], w_rcv.at[i, chip], seq=mate)
        for chip in range(n_chip)
        for i, hbm in enumerate((wc_hbm, wg_hbm))
    ]
    for copy in w_out_copies:
        copy.start()
    wo_copy.start()

    raw[pl.ds(m, 1)] = tok_ref[...][None]
    for k in range(1, n_mp):

        @pl.when(m - k >= 0)
        def _():
            b = m - k
            right_copy(raw.at[b], b, 0).wait_recv()

            @pl.when(m < n_mp - 1)
            def _():
                right_copy(raw.at[b], b, k).start()

        @pl.when(m + k <= n_mp - 1)
        def _():
            b = m + k
            left_copy(raw.at[b], b, 0).wait_recv()

            @pl.when(m > 0)
            def _():
                left_copy(raw.at[b], b, k).start()

    group = 16

    @pl.loop(0, rows // group)
    def _(i):
        at = pl.ds(pl.multiple_of(i * group, group), group)
        total = jnp.zeros((group, 1), jnp.float32)
        for b in range(n_mp):
            wide = raw[b, at, :].astype(jnp.float32)
            total = total + jnp.sum(wide * wide, axis=1, keepdims=True)
        factor = lax.rsqrt(total / (width * n_mp) + 1e-05)
        for b in range(n_mp):
            wide = raw[b, at, :].astype(jnp.float32)
            nsend[b, at, :] = (wide * factor * gain_ref[:, b * width : (b + 1) * width]).astype(jnp.bfloat16)

    def block(seq):
        return pl.ds(pl.multiple_of(seq * rows, rows), rows)

    scatter = []
    for o in range(1, n_chip):
        chip = (c + o) % n_chip
        scatter.append(
            remote(nsend.at[chip], xk.at[block(s)], k_snd.at[o], k_rcv.at[s], seq=chip * CORES + r)
        )
    scatter.append(remote(nsend.at[c], xk.at[block(s)], k_snd.at[0], k_rcv.at[s], seq=mate))
    for copy in scatter:
        copy.start()
    xk[block(s), :] = nsend[pl.ds(c, 1)].reshape(rows, width)
    forward = []
    for o in range(1, n_chip):
        there = ((c + n_chip - o) % n_chip) * CORES + r
        remote(nsend.at[c], xk.at[block(there)], k_snd.at[0], k_rcv.at[there], seq=mate).wait_recv()
        copy = remote(xk.at[block(there)], xk.at[block(there)], f_snd.at[o], k_rcv.at[there], seq=mate)
        copy.start()
        forward.append(copy)
    for copy in local:
        copy.wait()
    for copy in w_out_copies:
        copy.wait()
    for o in range(n_chip):
        there = ((c + n_chip - o) % n_chip) * CORES + (1 - r)
        remote(nsend.at[c], xk.at[block(there)], k_snd.at[0], k_rcv.at[there], seq=mate).wait_recv()

    step = 256
    partial = []
    for o in list(range(1, n_chip)) + [0]:
        chip = (c + o) % n_chip

        @pl.loop(0, tokens // step)
        def _(i):
            at = pl.ds(pl.multiple_of(i * step, step), step)
            value = jnp.dot(xk[at, :], wk[chip], preferred_element_type=jnp.float32)
            if o == 0:
                own[at, :] = value
            else:
                psend[o - 1, at, :] = value.astype(jnp.bfloat16)

        if o > 0:
            copy = remote(
                psend.at[o - 1], precv.at[o - 1], p_snd.at[o - 1], p_rcv.at[o - 1], seq=chip * CORES + r
            )
            copy.start()
            partial.append(copy)
    bias = bg_ref[pl.ds(q, 1), :]
    rec_gate = rg_ref[pl.ds(q, 1), :]
    rec_cand = rc_ref[pl.ds(q, 1), :]
    for copy in partial:
        copy.wait_recv()

    @pl.loop(0, tokens // group)
    def _(i):
        at = pl.ds(pl.multiple_of(i * group, group), group)
        value = own[at, :]
        for o in range(n_chip - 1):
            value = value + precv[o, at, :].astype(jnp.float32)
        cand_n[at, :] = value[:, :LANES]
        gate_n[at, :] = value[:, LANES:] + bias

    for newton_step in range(NEWTON):
        entering = jnp.zeros((n_seq, LANES), jnp.float32) if newton_step == 0 else carry[...]

        def lap(j, held):
            previous, a, b = held
            cand_pre = cand_n[pl.ds(j, n_seq, stride=rows), :]
            gate_pre = gate_n[pl.ds(j, n_seq, stride=rows), :]
            value, slope = cell(previous, cand_pre, gate_pre, rec_gate, rec_cand, 0.0)
            offset = value - slope * previous
            if newton_step > 0:
                previous = sweep_a[j] * entering + sweep_b[j]
            a, b = (slope * a, slope * b + offset)
            sweep_a[j] = a
            sweep_b[j] = b
            return (previous, a, b)

        zero = jnp.zeros((n_seq, LANES), jnp.float32)
        _, a, b = lax.fori_loop(0, rows, lap, (entering, zero + 1.0, zero), unroll=8)
        state = jnp.zeros((1, LANES), jnp.float32)
        for i in range(n_seq):
            carry[i : i + 1, :] = state
            state = a[i : i + 1, :] * state + b[i : i + 1, :]
    entering = carry[...]

    @pl.loop(0, rows, unroll=8)
    def _(j):
        cand_n[pl.ds(j, n_seq, stride=rows), :] = sweep_a[j] * entering + sweep_b[j]

    for i in range(n_seq):
        ssend[i] = cand_n[i * rows : (i + 1) * rows, :].astype(jnp.bfloat16)
    lane = pl.ds(pl.multiple_of(q * LANES, LANES), LANES)
    spread = []
    for o in range(1, n_seq):
        there = (s + o) % n_seq
        copy = remote(ssend.at[there], sall.at[:, lane], s_snd.at[o], s_rcv.at[o], seq=there)
        copy.start()
        spread.append(copy)
    sall[:, lane] = ssend[pl.ds(s, 1)].reshape(rows, LANES)
    wo_copy.wait()
    for copy in spread:
        copy.wait_recv()

    cols = out_ref.shape[1]
    for d in range(n_mp):
        pout[d] = jnp.dot(sall[...], wo[:, d * cols : (d + 1) * cols], preferred_element_type=jnp.float32)

    def hop(side, d):
        there = (m + 1) % n_mp if side == 0 else (m + n_mp - 1) % n_mp
        return remote(osend.at[d], orecv.at[side, d], o_snd.at[d], o_rcv.at[side, d], mp=there)

    for k in range(n_mp - 1, 0, -1):
        for side, sign in ((0, 1), (1, -1)):
            d = m + sign * k
            inside = (d <= n_mp - 1) if side == 0 else (d >= 0)
            first = (m == 0) if side == 0 else (m == n_mp - 1)

            @pl.when(inside & first)
            def _():
                osend[d] = pout[d].astype(jnp.bfloat16)
                hop(side, d).start()

            @pl.when(inside & jnp.logical_not(first))
            def _():
                hop(side, d).wait_recv()
                osend[d] = (pout[d] + orecv[side, d].astype(jnp.float32)).astype(jnp.bfloat16)
                hop(side, d).start()

    @pl.when(m > 0)
    def _():
        hop(0, m).wait_recv()
        pout[m] = pout[m] + orecv[0, m].astype(jnp.float32)

    @pl.when(m < n_mp - 1)
    def _():
        hop(1, m).wait_recv()
        pout[m] = pout[m] + orecv[1, m].astype(jnp.float32)

    out_ref[...] = pout[m].astype(jnp.bfloat16)

    for k in range(n_mp - 1):

        @pl.when((m < n_mp - 1) & (m - k >= 0))
        def _():
            right_copy(raw.at[m - k], m - k, k).wait_send()

        @pl.when((m > 0) & (m + k <= n_mp - 1))
        def _():
            left_copy(raw.at[m + k], m + k, k).wait_send()

    for copy in scatter + forward + partial + spread:
        copy.wait_send()
    for d in range(n_mp):

        @pl.when(d != m)
        def _():
            hop(0, d).wait_send()


def fused(n_seq, n_mp, tokens, norm_gain, w_cand, w_gate, rec_gate, rec_cand, bias_gate, w_out):
    rows, width = tokens.shape
    k_own, channels = w_cand.shape
    n_chip = n_seq // CORES
    length = rows * n_seq
    bf16, f32 = (jnp.bfloat16, jnp.float32)
    vmem, dma = (pltpu.VMEM, pltpu.SemaphoreType.DMA)
    whole = pl.BlockSpec(memory_space=pltpu.VMEM)
    far = pl.BlockSpec(memory_space=pl.ANY)
    per_channel = [part.reshape(n_seq, LANES) for part in (rec_gate, rec_cand, bias_gate)]
    return pl.pallas_call(
        functools.partial(fused_kernel, n_seq, n_mp),
        out_shape=jax.ShapeDtypeStruct((rows, width), bf16),
        in_specs=[whole, whole, far, far, whole, whole, whole, far],
        out_specs=whole,
        scratch_shapes=[
            vmem((n_mp, rows, width), bf16),
            vmem((n_chip, rows, width), bf16),
            vmem((length, width), bf16),
            vmem((n_chip, k_own * CORES, 2 * LANES), bf16),
            vmem(w_out.shape, bf16),
            vmem((length, 2 * LANES), f32),
            vmem((n_chip - 1, length, 2 * LANES), bf16),
            vmem((n_chip - 1, length, 2 * LANES), bf16),
            vmem((length, LANES), f32),
            vmem((length, LANES), f32),
            vmem((rows, n_seq, LANES), f32),
            vmem((rows, n_seq, LANES), f32),
            vmem((n_seq, LANES), f32),
            vmem((n_seq, rows, LANES), bf16),
            vmem((rows, channels), bf16),
            vmem((n_mp, rows, width), f32),
            vmem((n_mp, rows, width), bf16),
            vmem((2, n_mp, rows, width), bf16),
            dma((2, n_chip)),
            dma((2, n_chip)),
            dma((2, n_chip)),
            dma,
            dma((2, n_mp)),
            dma((n_mp,)),
            dma((n_chip,)),
            dma((n_seq,)),
            dma((n_chip,)),
            dma((n_chip,)),
            dma((n_chip,)),
            dma((n_seq,)),
            dma((n_seq,)),
            dma((n_mp,)),
            dma((2, n_mp)),
        ],
        compiler_params=pltpu.CompilerParams(collective_id=0, has_side_effects=True),
    )(tokens, norm_gain.reshape(1, -1), w_cand, w_gate, *per_channel, w_out)


def layer(n_seq, n_mp, *args):
    tokens, w_cand = (args[0], args[2])
    fits = (
        n_seq == SUBLANES
        and n_seq // CORES == n_mp
        and w_cand.shape[1] == n_seq * LANES
        and tokens.shape[0] % LANES == 0
        and tokens.shape[1] % LANES == 0
    )
    return fused(n_seq, n_mp, *args) if fits else per_device(*args)


def solution(mesh):
    placed = (
        P("seq", "mp"),
        P(),
        P("seq", "mp"),
        P("seq", "mp"),
        P("mp"),
        P("mp"),
        P("mp"),
        P("mp", None),
    )
    return jax.shard_map(
        functools.partial(layer, mesh.shape["seq"], mesh.shape["mp"]), mesh=mesh, in_specs=placed, out_specs=P("seq", "mp"), check_vma=False
    )
```

```python
import functools

import jax
import jax.numpy as jnp
from jax import lax
from jax.experimental import pallas as pl
from jax.experimental.pallas import tpu as pltpu
from jax.sharding import PartitionSpec as P

NEWTON = 3


def prefix(value, axis, join, neutral):
    count, mine = (lax.axis_size(axis), lax.axis_index(axis))
    pieces = jax.tree.map(lambda part: lax.all_gather(part, axis), value)
    subtotal = jax.tree.map(
        lambda part, zero: jnp.full_like(part, 0) + jnp.asarray(zero, part.dtype), value, neutral
    )

    def lap(position, subtotal):
        longer = join(subtotal, jax.tree.map(lambda part: part[position], pieces))
        return jax.tree.map(lambda new, old: jnp.where(position < mine, new, old), longer, subtotal)

    return lax.fori_loop(0, count - 1, lap, subtotal)


def compose(earlier, later):
    return (later[0] * earlier[0], later[0] * earlier[1] + later[1])


def cell(previous, cand_pre, gate_pre, rec_gate, rec_cand, bias_gate):
    gate = jax.nn.sigmoid(gate_pre + rec_gate * previous + bias_gate)
    cand = jnp.tanh(cand_pre + rec_cand * previous)
    value = gate * previous + (1.0 - gate) * cand
    slope = (
        gate
        + gate * (1.0 - gate) * rec_gate * (previous - cand)
        + (1.0 - gate) * (1.0 - cand * cand) * rec_cand
    )
    return (value, slope)


def per_device(tokens, norm_gain, w_cand, w_gate, rec_gate, rec_cand, bias_gate, w_out):
    tok_rows = tokens.shape[0]
    channels = w_cand.shape[1]
    whole = lax.all_gather(tokens, "mp", axis=1, tiled=True)
    wide = whole.astype(jnp.float32)
    factor = lax.rsqrt(jnp.mean(wide * wide, axis=1, keepdims=True) + 1e-05)
    normed = (wide * factor * norm_gain).astype(jnp.bfloat16)
    cand_pre = jnp.dot(
        normed,
        lax.all_gather(w_cand, "seq", axis=0, tiled=True),
        preferred_element_type=jnp.float32,
    )
    gate_pre = jnp.dot(
        normed,
        lax.all_gather(w_gate, "seq", axis=0, tiled=True),
        preferred_element_type=jnp.float32,
    )
    state = jnp.zeros((tok_rows, channels), jnp.float32)
    carried = jnp.zeros((channels,), jnp.float32)
    ones_row = jnp.ones((channels,), jnp.float32)
    for newton_step in range(NEWTON):
        previous = jnp.concatenate([carried[None, :], state[:-1]], axis=0)
        value, slope = cell(previous, cand_pre, gate_pre, rec_gate, rec_cand, bias_gate)
        offset = value - slope * previous
        sweep_a, sweep_b = lax.associative_scan(compose, (slope, offset), axis=0)
        entering = prefix((sweep_a[-1], sweep_b[-1]), "seq", compose, (ones_row, carried * 0.0))
        carried = entering[1]
        state = sweep_a * carried + sweep_b
    state_b = state.astype(jnp.bfloat16)
    partial_sums = jnp.dot(state_b, w_out, preferred_element_type=jnp.float32)
    summed = lax.psum_scatter(partial_sums, "mp", scatter_dimension=1, tiled=True)
    return summed.astype(jnp.bfloat16)


CORES = 2
SUBLANES = 8
LANES = 128
PIECES = 4
HALVES = 2
GROUP = 16
MESH = pl.DeviceIdType.MESH


def fused_kernel(
    n_seq,
    n_mp,
    tok_ref,
    gain_ref,
    wc_hbm,
    wg_hbm,
    rg_ref,
    rc_ref,
    bg_ref,
    wo_hbm,
    out_ref,
    raw,
    xk,
    xn,
    sq_own,
    sq_all,
    f_own,
    f_all,
    f_col,
    wk,
    wo,
    own,
    psend,
    precv,
    cand_n,
    gate_n,
    sweep_a,
    sweep_b,
    carry,
    ssend,
    sall,
    pout,
    osend,
    orecv,
    w_loc,
    w_snd,
    w_rcv,
    wo_sem,
    z_snd,
    z_rcv,
    k_snd,
    k_rcv,
    f_snd,
    q_snd,
    q_rcv,
    g_snd,
    g_rcv,
    p_snd,
    p_rcv,
    s_snd,
    s_rcv,
    o_snd,
    o_rcv,
):
    s, m = (lax.axis_index("seq"), lax.axis_index("mp"))
    n_chip = n_seq // CORES
    c, r = (s // CORES, s % CORES)
    mate = c * CORES + (1 - r)
    rows = tok_ref.shape[0]
    tokens = rows * n_seq
    k_own = wc_hbm.shape[0]
    width = raw.shape[2]
    q = r * n_chip + c

    def remote(src, dst, snd, rcv, **where):
        return pltpu.make_async_remote_copy(
            src_ref=src, dst_ref=dst, send_sem=snd, recv_sem=rcv, device_id=where, device_id_type=MESH
        )

    def barrier():
        sem = pltpu.get_barrier_semaphore()
        for o in range(1, n_seq):
            pl.semaphore_signal(sem, inc=1, device_id={"seq": (s + o) % n_seq}, device_id_type=MESH)
        for o in range(1, n_mp):
            pl.semaphore_signal(sem, inc=1, device_id={"mp": (m + o) % n_mp}, device_id_type=MESH)
        pl.semaphore_wait(sem, n_seq + n_mp - 2)

    def w_piece(hbm, core, chip):
        return hbm.at[:, pl.ds(pl.multiple_of((core * n_chip + chip) * LANES, LANES), LANES)]

    def w_place(i, chip, core):
        return wk.at[chip, pl.ds(pl.multiple_of(core * k_own, k_own), k_own), pl.ds(i * LANES, LANES)]

    local = [
        pltpu.make_async_copy(w_piece(hbm, r, chip), w_place(i, chip, r), w_loc.at[i, chip])
        for chip in range(n_chip)
        for i, hbm in enumerate((wc_hbm, wg_hbm))
    ]
    wo_copy = pltpu.make_async_copy(wo_hbm, wo, wo_sem)
    for copy in local:
        copy.start()
    barrier()

    part = rows // PIECES

    def piece(p):
        return pl.ds(p * part, part)

    def place(p, seq):
        return pl.ds(pl.multiple_of((p * n_seq + seq) * part, part), part)

    def z_copy(side, src, b, p, k):
        there = (m + 1) % n_mp if side == 0 else (m + n_mp - 1) % n_mp
        return remote(src, raw.at[b, piece(p)], z_snd.at[side, k, p], z_rcv.at[b, p], mp=there)

    def not_last(side):
        return m < n_mp - 1 if side == 0 else m > 0

    def plane_copy(src, b, p):
        seq = jnp.where(b == c, mate, b * CORES + r)
        return remote(src, xk.at[place(p, s)], k_snd.at[b, p], k_rcv.at[p, s], seq=seq)

    def send_own(p):
        mine = tok_ref.at[piece(p)]
        for side in range(2):

            @pl.when(not_last(side))
            def _():
                z_copy(side, mine, m, p, 0).start()

        plane_copy(mine, m, p).start()

        @pl.when(m == c)
        def _():
            xk[place(p, s), :] = tok_ref[piece(p), :]

    def pass_on(p, k):
        for side, sign in ((0, -1), (1, 1)):
            b = m + sign * k

            @pl.when((b >= 0) & (b <= n_mp - 1))
            def _():
                here = raw.at[b, piece(p)]
                z_copy(side, here, b, p, 0).wait_recv()

                @pl.when(not_last(side))
                def _():
                    z_copy(side, here, b, p, k).start()

                plane_copy(here, b, p).start()

                @pl.when(b == c)
                def _():
                    xk[place(p, s), :] = raw[b, piece(p), :]

    for p in range(min(2, PIECES)):
        send_own(p)

    across = lax.broadcasted_iota(jnp.int32, (rows, rows), 0) == lax.broadcasted_iota(
        jnp.int32, (rows, rows), 1
    )
    wide = tok_ref[...].astype(jnp.float32)
    squares = jnp.sum(wide * wide, axis=1, keepdims=True)
    squares = jnp.sum(jnp.where(across, squares, 0.0), axis=0, keepdims=True)
    sq_own[...] = jnp.broadcast_to(squares, sq_own.shape)
    sq_copies = []
    for o in range(1, n_mp):
        copy = remote(sq_own, sq_all.at[o], q_snd.at[o], q_rcv.at[o], mp=(m + o) % n_mp)
        copy.start()
        sq_copies.append(copy)

    w_out_copies = [
        remote(w_piece(hbm, 1 - r, chip), w_place(i, chip, r), w_snd.at[i, chip], w_rcv.at[i, chip], seq=mate)
        for chip in range(n_chip)
        for i, hbm in enumerate((wc_hbm, wg_hbm))
    ]
    for copy in w_out_copies:
        copy.start()
    wo_copy.start()
    gain = gain_ref[pl.ds(c, 1), :]
    bias = bg_ref[pl.ds(q, 1), :]
    rec_gate = rg_ref[pl.ds(q, 1), :]
    rec_cand = rc_ref[pl.ds(q, 1), :]
    tile = n_seq * part
    forward, partial, f_copies = ([], [], [])

    def stage_a(p):
        for k in range(1, n_mp):
            pass_on(p, k)
            if k == 1 and p + 2 < PIECES:
                send_own(p + 2)

    def factors():
        total = sq_own[...]
        for copy in sq_copies:
            copy.wait_recv()
        for o in range(1, n_mp):
            total = total + sq_all[o]
        f_own[...] = lax.rsqrt(total / (width * n_mp) + 1e-05)
        for o in range(1, n_seq):
            copy = remote(f_own, f_all.at[s], g_snd.at[o], g_rcv.at[s], seq=(s + o) % n_seq)
            copy.start()
            f_copies.append(copy)
        f_all[pl.ds(s, 1)] = f_own[...][None]

    def spread_factors():
        for o in range(1, n_seq):
            there = (s + o) % n_seq
            remote(f_own, f_all.at[there], g_snd.at[o], g_rcv.at[there], seq=there).wait_recv()
        for i in range(n_seq):
            row = f_all[i, 0:1, :]
            column = jnp.sum(jnp.where(across, row, 0.0), axis=1, keepdims=True)
            column = jnp.broadcast_to(column, (rows, LANES))
            for p in range(PIECES):
                f_col[(p * n_seq + i) * part : (p * n_seq + i + 1) * part, :] = column[
                    p * part : (p + 1) * part, :
                ]

    def arrived(p, seq):
        remote(tok_ref.at[piece(p)], xk.at[place(p, seq)], k_snd.at[0, p], k_rcv.at[p, seq], seq=mate).wait_recv()

    def stage_b(p):
        for o in range(1, n_chip):
            there = ((c + n_chip - o) % n_chip) * CORES + r
            arrived(p, there)
            copy = remote(
                xk.at[place(p, there)], xk.at[place(p, there)], f_snd.at[o, p], k_rcv.at[p, there], seq=mate
            )
            copy.start()
            forward.append(copy)

    def stage_c(p):
        for o in range(n_chip):
            arrived(p, ((c + n_chip - o) % n_chip) * CORES + (1 - r))

        @pl.loop(0, tile // GROUP)
        def _(i):
            at = pl.ds(pl.multiple_of(i * GROUP, GROUP), GROUP)
            of = pl.ds(pl.multiple_of(p * tile + i * GROUP, GROUP), GROUP)
            xn[at, :] = (xk[of, :].astype(jnp.float32) * f_col[of, 0:1] * gain).astype(jnp.bfloat16)

        at = pl.ds(p * tile, tile)
        for o in list(range(1, n_chip)) + [0]:
            chip = (c + o) % n_chip
            value = jnp.dot(xn[...], wk[chip], preferred_element_type=jnp.float32)
            if o == 0:
                own[at, :] = value
            else:
                psend[o - 1, at, :] = value.astype(jnp.bfloat16)
                copy = remote(
                    psend.at[o - 1, at],
                    precv.at[o - 1, at],
                    p_snd.at[o, p],
                    p_rcv.at[o, p],
                    seq=chip * CORES + r,
                )
                copy.start()
                partial.append(copy)

    for turn in range(PIECES + 2):
        if turn < PIECES:
            stage_a(turn)
        if turn == 0:
            factors()
        if 0 <= turn - 1 < PIECES:
            stage_b(turn - 1)
        if turn == 1:
            spread_factors()
            for copy in local:
                copy.wait()
            for copy in w_out_copies:
                copy.wait()
        if 0 <= turn - 2 < PIECES:
            stage_c(turn - 2)

    def gather_piece(p):
        for copy in partial[p * (n_chip - 1) : (p + 1) * (n_chip - 1)]:
            copy.wait_recv()

        @pl.loop(0, tile // GROUP)
        def _(i):
            at = pl.ds(pl.multiple_of(p * tile + i * GROUP, GROUP), GROUP)
            value = own[at, :]
            for o in range(n_chip - 1):
                value = value + precv[o, at, :].astype(jnp.float32)
            cand_n[at, :] = value[:, :LANES]
            gate_n[at, :] = value[:, LANES:] + bias

    for newton_step in range(NEWTON):
        zero = jnp.zeros((n_seq, LANES), jnp.float32)
        entering = zero if newton_step == 0 else carry[...]
        held = (entering, zero + 1.0, zero)
        for p in range(PIECES):
            if newton_step == 0:
                gather_piece(p)

            def lap(i, held):
                previous, a, b = held
                j = p * part + i
                at = pl.ds(p * tile + i, n_seq, stride=part)
                value, slope = cell(previous, cand_n[at, :], gate_n[at, :], rec_gate, rec_cand, 0.0)
                offset = value - slope * previous
                if newton_step > 0:
                    previous = sweep_a[j] * entering + sweep_b[j]
                a, b = (slope * a, slope * b + offset)
                sweep_a[j] = a
                sweep_b[j] = b
                return (previous, a, b)

            held = lax.fori_loop(0, part, lap, held, unroll=8)
        _, a, b = held
        state = jnp.zeros((1, LANES), jnp.float32)
        for i in range(n_seq):
            carry[i : i + 1, :] = state
            state = a[i : i + 1, :] * state + b[i : i + 1, :]
    entering = carry[...]
    for p in range(PIECES):

        @pl.loop(0, part, unroll=8)
        def _(i):
            j = p * part + i
            cand_n[pl.ds(p * tile + i, n_seq, stride=part), :] = sweep_a[j] * entering + sweep_b[j]

    for i in range(n_seq):
        for p in range(PIECES):
            start = (p * n_seq + i) * part
            ssend[i, p * part : (p + 1) * part, :] = cand_n[start : start + part, :].astype(jnp.bfloat16)
    lane = pl.ds(pl.multiple_of(q * LANES, LANES), LANES)
    spread = []
    for o in range(1, n_seq):
        there = (s + o) % n_seq
        copy = remote(ssend.at[there], sall.at[:, lane], s_snd.at[o], s_rcv.at[o], seq=there)
        copy.start()
        spread.append(copy)
    sall[:, lane] = ssend[pl.ds(s, 1)].reshape(rows, LANES)
    wo_copy.wait()
    for copy in spread:
        copy.wait_recv()

    cols = out_ref.shape[1]
    half = rows // HALVES

    def hop(side, d, h):
        there = (m + 1) % n_mp if side == 0 else (m + n_mp - 1) % n_mp
        at = pl.ds(h * half, half)
        return remote(
            osend.at[d, at], orecv.at[side, d, at], o_snd.at[d, h], o_rcv.at[side, d, h], mp=there
        )

    def project(d):
        lanes = pl.ds(pl.multiple_of(d * cols, cols), cols)
        pout[...] = jnp.dot(sall[...], wo[:, lanes], preferred_element_type=jnp.float32)

    for k in range(n_mp - 1, 0, -1):
        for side, sign in ((0, 1), (1, -1)):
            d = m + sign * k
            inside = (d <= n_mp - 1) if side == 0 else (d >= 0)
            first = (m == 0) if side == 0 else (m == n_mp - 1)

            @pl.when(inside)
            def _():
                project(d)
                for h in range(HALVES):
                    at = pl.ds(h * half, half)

                    @pl.when(first)
                    def _():
                        osend[d, at, :] = pout[at, :].astype(jnp.bfloat16)

                    @pl.when(jnp.logical_not(first))
                    def _():
                        hop(side, d, h).wait_recv()
                        osend[d, at, :] = (pout[at, :] + orecv[side, d, at, :].astype(jnp.float32)).astype(
                            jnp.bfloat16
                        )

                    hop(side, d, h).start()

    project(m)
    for side in range(2):

        @pl.when(m > 0 if side == 0 else m < n_mp - 1)
        def _():
            for h in range(HALVES):
                at = pl.ds(h * half, half)
                hop(side, m, h).wait_recv()
                pout[at, :] = pout[at, :] + orecv[side, m, at, :].astype(jnp.float32)

    out_ref[...] = pout[...].astype(jnp.bfloat16)

    for p in range(PIECES):
        for k in range(n_mp):
            for side, sign in ((0, -1), (1, 1)):
                b = m + sign * k

                @pl.when(not_last(side) & (b >= 0) & (b <= n_mp - 1))
                def _():
                    z_copy(side, tok_ref.at[piece(p)], b, p, k).wait_send()

            plane_copy(tok_ref.at[piece(p)], k, p).wait_send()

    for copy in sq_copies + f_copies + forward + partial + spread:
        copy.wait_send()
    for d in range(n_mp):

        @pl.when(d != m)
        def _():
            for h in range(HALVES):
                hop(0, d, h).wait_send()


def fused(n_seq, n_mp, tokens, norm_gain, w_cand, w_gate, rec_gate, rec_cand, bias_gate, w_out):
    rows, width = tokens.shape
    k_own, channels = w_cand.shape
    n_chip = n_seq // CORES
    length = rows * n_seq
    bf16, f32 = (jnp.bfloat16, jnp.float32)
    vmem, dma = (pltpu.VMEM, pltpu.SemaphoreType.DMA)
    whole = pl.BlockSpec(memory_space=pltpu.VMEM)
    far = pl.BlockSpec(memory_space=pl.ANY)
    per_channel = [part.reshape(n_seq, LANES) for part in (rec_gate, rec_cand, bias_gate)]
    return pl.pallas_call(
        functools.partial(fused_kernel, n_seq, n_mp),
        out_shape=jax.ShapeDtypeStruct((rows, width), bf16),
        in_specs=[whole, whole, far, far, whole, whole, whole, far],
        out_specs=whole,
        scratch_shapes=[
            vmem((n_mp, rows, width), bf16),
            vmem((length, width), bf16),
            vmem((length // PIECES, width), bf16),
            vmem((n_seq, LANES), f32),
            vmem((n_mp, n_seq, LANES), f32),
            vmem((n_seq, LANES), f32),
            vmem((n_seq, n_seq, LANES), f32),
            vmem((length, LANES), f32),
            vmem((n_chip, k_own * CORES, 2 * LANES), bf16),
            vmem(w_out.shape, bf16),
            vmem((length, 2 * LANES), f32),
            vmem((n_chip - 1, length, 2 * LANES), bf16),
            vmem((n_chip - 1, length, 2 * LANES), bf16),
            vmem((length, LANES), f32),
            vmem((length, LANES), f32),
            vmem((rows, n_seq, LANES), f32),
            vmem((rows, n_seq, LANES), f32),
            vmem((n_seq, LANES), f32),
            vmem((n_seq, rows, LANES), bf16),
            vmem((rows, channels), bf16),
            vmem((rows, width), f32),
            vmem((n_mp, rows, width), bf16),
            vmem((2, n_mp, rows, width), bf16),
            dma((2, n_chip)),
            dma((2, n_chip)),
            dma((2, n_chip)),
            dma,
            dma((2, n_mp, PIECES)),
            dma((n_mp, PIECES)),
            dma((n_mp, PIECES)),
            dma((PIECES, n_seq)),
            dma((n_chip, PIECES)),
            dma((n_mp,)),
            dma((n_mp,)),
            dma((n_seq,)),
            dma((n_seq,)),
            dma((n_chip, PIECES)),
            dma((n_chip, PIECES)),
            dma((n_seq,)),
            dma((n_seq,)),
            dma((n_mp, HALVES)),
            dma((2, n_mp, HALVES)),
        ],
        compiler_params=pltpu.CompilerParams(collective_id=0, has_side_effects=True),
    )(tokens, norm_gain.reshape(n_mp, -1), w_cand, w_gate, *per_channel, w_out)


def layer(n_seq, n_mp, *args):
    tokens, w_cand = (args[0], args[2])
    fits = (
        n_seq == SUBLANES
        and n_seq // CORES == n_mp
        and w_cand.shape[1] == n_seq * LANES
        and tokens.shape[0] == LANES
        and tokens.shape[1] % LANES == 0
    )
    return fused(n_seq, n_mp, *args) if fits else per_device(*args)


def solution(mesh):
    placed = (
        P("seq", "mp"),
        P(),
        P("seq", "mp"),
        P("seq", "mp"),
        P("mp"),
        P("mp"),
        P("mp"),
        P("mp", None),
    )
    return jax.shard_map(
        functools.partial(layer, mesh.shape["seq"], mesh.shape["mp"]), mesh=mesh, in_specs=placed, out_specs=P("seq", "mp"), check_vma=False
    )
```

```python
import functools

import jax
import jax.numpy as jnp
from jax import lax
from jax.experimental import pallas as pl
from jax.experimental.pallas import tpu as pltpu
from jax.sharding import PartitionSpec as P

NEWTON = 3


def prefix(value, axis, join, neutral):
    count, mine = (lax.axis_size(axis), lax.axis_index(axis))
    pieces = jax.tree.map(lambda part: lax.all_gather(part, axis), value)
    subtotal = jax.tree.map(
        lambda part, zero: jnp.full_like(part, 0) + jnp.asarray(zero, part.dtype), value, neutral
    )

    def lap(position, subtotal):
        longer = join(subtotal, jax.tree.map(lambda part: part[position], pieces))
        return jax.tree.map(lambda new, old: jnp.where(position < mine, new, old), longer, subtotal)

    return lax.fori_loop(0, count - 1, lap, subtotal)


def compose(earlier, later):
    return (later[0] * earlier[0], later[0] * earlier[1] + later[1])


def cell(previous, cand_pre, gate_pre, rec_gate, rec_cand, bias_gate):
    gate = jax.nn.sigmoid(gate_pre + rec_gate * previous + bias_gate)
    cand = jnp.tanh(cand_pre + rec_cand * previous)
    value = gate * previous + (1.0 - gate) * cand
    slope = (
        gate
        + gate * (1.0 - gate) * rec_gate * (previous - cand)
        + (1.0 - gate) * (1.0 - cand * cand) * rec_cand
    )
    return (value, slope)


def per_device(tokens, norm_gain, w_cand, w_gate, rec_gate, rec_cand, bias_gate, w_out):
    tok_rows = tokens.shape[0]
    channels = w_cand.shape[1]
    whole = lax.all_gather(tokens, "mp", axis=1, tiled=True)
    wide = whole.astype(jnp.float32)
    factor = lax.rsqrt(jnp.mean(wide * wide, axis=1, keepdims=True) + 1e-05)
    normed = (wide * factor * norm_gain).astype(jnp.bfloat16)
    cand_pre = jnp.dot(
        normed,
        lax.all_gather(w_cand, "seq", axis=0, tiled=True),
        preferred_element_type=jnp.float32,
    )
    gate_pre = jnp.dot(
        normed,
        lax.all_gather(w_gate, "seq", axis=0, tiled=True),
        preferred_element_type=jnp.float32,
    )
    state = jnp.zeros((tok_rows, channels), jnp.float32)
    carried = jnp.zeros((channels,), jnp.float32)
    ones_row = jnp.ones((channels,), jnp.float32)
    for newton_step in range(NEWTON):
        previous = jnp.concatenate([carried[None, :], state[:-1]], axis=0)
        value, slope = cell(previous, cand_pre, gate_pre, rec_gate, rec_cand, bias_gate)
        offset = value - slope * previous
        sweep_a, sweep_b = lax.associative_scan(compose, (slope, offset), axis=0)
        entering = prefix((sweep_a[-1], sweep_b[-1]), "seq", compose, (ones_row, carried * 0.0))
        carried = entering[1]
        state = sweep_a * carried + sweep_b
    state_b = state.astype(jnp.bfloat16)
    partial_sums = jnp.dot(state_b, w_out, preferred_element_type=jnp.float32)
    summed = lax.psum_scatter(partial_sums, "mp", scatter_dimension=1, tiled=True)
    return summed.astype(jnp.bfloat16)


CORES = 2
SUBLANES = 8
LANES = 128
PIECES = 4
HALVES = 2
GROUP = 16
MESH = pl.DeviceIdType.MESH


def fused_kernel(
    n_seq,
    n_mp,
    tok_ref,
    gain_ref,
    wc_hbm,
    wg_hbm,
    rg_ref,
    rc_ref,
    bg_ref,
    wo_hbm,
    out_ref,
    raw,
    xk,
    xn,
    sq_own,
    sq_all,
    f_own,
    f_all,
    f_col,
    wk,
    wo,
    own,
    onward,
    psend,
    precv,
    cand_n,
    gate_n,
    sweep_a,
    sweep_b,
    carry,
    ssend,
    sall,
    pout,
    osend,
    orecv,
    w_loc,
    w_snd,
    w_rcv,
    wo_sem,
    z_snd,
    z_rcv,
    k_snd,
    k_rcv,
    f_snd,
    q_snd,
    q_rcv,
    g_snd,
    g_rcv,
    p_snd,
    p_rcv,
    s_snd,
    s_rcv,
    o_snd,
    o_rcv,
):
    s, m = (lax.axis_index("seq"), lax.axis_index("mp"))
    n_chip = n_seq // CORES
    c, r = (s // CORES, s % CORES)
    mate = c * CORES + (1 - r)
    rows = tok_ref.shape[0]
    tokens = rows * n_seq
    k_own = wc_hbm.shape[0]
    width = raw.shape[2]
    q = r * n_chip + c

    def remote(src, dst, snd, rcv, **where):
        return pltpu.make_async_remote_copy(
            src_ref=src, dst_ref=dst, send_sem=snd, recv_sem=rcv, device_id=where, device_id_type=MESH
        )

    def barrier():
        sem = pltpu.get_barrier_semaphore()
        for o in range(1, n_seq):
            pl.semaphore_signal(sem, inc=1, device_id={"seq": (s + o) % n_seq}, device_id_type=MESH)
        for o in range(1, n_mp):
            pl.semaphore_signal(sem, inc=1, device_id={"mp": (m + o) % n_mp}, device_id_type=MESH)
        pl.semaphore_wait(sem, n_seq + n_mp - 2)

    def w_piece(hbm, core, chip):
        return hbm.at[:, pl.ds(pl.multiple_of((core * n_chip + chip) * LANES, LANES), LANES)]

    def w_place(i, chip, core):
        return wk.at[chip, pl.ds(pl.multiple_of(core * k_own, k_own), k_own), pl.ds(i * LANES, LANES)]

    local = [
        pltpu.make_async_copy(w_piece(hbm, r, chip), w_place(i, chip, r), w_loc.at[i, chip])
        for chip in range(n_chip)
        for i, hbm in enumerate((wc_hbm, wg_hbm))
    ]
    wo_copy = pltpu.make_async_copy(wo_hbm, wo, wo_sem)
    for copy in local:
        copy.start()
    barrier()

    part = rows // PIECES

    def piece(p):
        return pl.ds(p * part, part)

    def place(p, seq):
        return pl.ds(pl.multiple_of((p * n_seq + seq) * part, part), part)

    def z_copy(side, src, b, p, k):
        there = (m + 1) % n_mp if side == 0 else (m + n_mp - 1) % n_mp
        return remote(src, raw.at[b, piece(p)], z_snd.at[side, k, p], z_rcv.at[b, p], mp=there)

    def not_last(side):
        return m < n_mp - 1 if side == 0 else m > 0

    def plane_copy(src, b, p):
        seq = jnp.where(b == c, mate, b * CORES + r)
        return remote(src, xk.at[place(p, s)], k_snd.at[b, p], k_rcv.at[p, s], seq=seq)

    def send_own(p):
        mine = tok_ref.at[piece(p)]
        for side in range(2):

            @pl.when(not_last(side))
            def _():
                z_copy(side, mine, m, p, 0).start()

        plane_copy(mine, m, p).start()

        @pl.when(m == c)
        def _():
            xk[place(p, s), :] = tok_ref[piece(p), :]

    def pass_on(p, k):
        for side, sign in ((0, -1), (1, 1)):
            b = m + sign * k

            @pl.when((b >= 0) & (b <= n_mp - 1))
            def _():
                here = raw.at[b, piece(p)]
                z_copy(side, here, b, p, 0).wait_recv()

                @pl.when(not_last(side))
                def _():
                    z_copy(side, here, b, p, k).start()

                plane_copy(here, b, p).start()

                @pl.when(b == c)
                def _():
                    xk[place(p, s), :] = raw[b, piece(p), :]

    for p in range(min(2, PIECES)):
        send_own(p)

    across = lax.broadcasted_iota(jnp.int32, (rows, rows), 0) == lax.broadcasted_iota(
        jnp.int32, (rows, rows), 1
    )
    wide = tok_ref[...].astype(jnp.float32)
    squares = jnp.sum(wide * wide, axis=1, keepdims=True)
    squares = jnp.sum(jnp.where(across, squares, 0.0), axis=0, keepdims=True)
    sq_own[...] = jnp.broadcast_to(squares, sq_own.shape)
    sq_copies = []
    for o in range(1, n_mp):
        copy = remote(sq_own, sq_all.at[o], q_snd.at[o], q_rcv.at[o], mp=(m + o) % n_mp)
        copy.start()
        sq_copies.append(copy)

    w_out_copies = [
        remote(w_piece(hbm, 1 - r, chip), w_place(i, chip, r), w_snd.at[i, chip], w_rcv.at[i, chip], seq=mate)
        for chip in range(n_chip)
        for i, hbm in enumerate((wc_hbm, wg_hbm))
    ]
    for copy in w_out_copies:
        copy.start()
    wo_copy.start()
    gain = gain_ref[pl.ds(c, 1), :]
    bias = bg_ref[pl.ds(q, 1), :]
    rec_gate = rg_ref[pl.ds(q, 1), :]
    rec_cand = rc_ref[pl.ds(q, 1), :]
    tile = n_seq * part
    forward, f_copies = ([], [])

    def stage_a(turn):
        if turn + 2 < PIECES:
            send_own(turn + 2)
        for k in range(1, n_mp):
            p = turn - (k - 1)
            if 0 <= p < PIECES:
                pass_on(p, k)

    def factors():
        total = sq_own[...]
        for copy in sq_copies:
            copy.wait_recv()
        for o in range(1, n_mp):
            total = total + sq_all[o]
        f_own[...] = lax.rsqrt(total / (width * n_mp) + 1e-05)
        for o in range(1, n_seq):
            copy = remote(f_own, f_all.at[s], g_snd.at[o], g_rcv.at[s], seq=(s + o) % n_seq)
            copy.start()
            f_copies.append(copy)
        f_all[pl.ds(s, 1)] = f_own[...][None]

    def spread_factors():
        for o in range(1, n_seq):
            there = (s + o) % n_seq
            remote(f_own, f_all.at[there], g_snd.at[o], g_rcv.at[there], seq=there).wait_recv()
        for i in range(n_seq):
            row = f_all[i, 0:1, :]
            column = jnp.sum(jnp.where(across, row, 0.0), axis=1, keepdims=True)
            column = jnp.broadcast_to(column, (rows, LANES))
            for p in range(PIECES):
                f_col[(p * n_seq + i) * part : (p * n_seq + i + 1) * part, :] = column[
                    p * part : (p + 1) * part, :
                ]

    def arrived(p, seq):
        remote(tok_ref.at[piece(p)], xk.at[place(p, seq)], k_snd.at[0, p], k_rcv.at[p, seq], seq=mate).wait_recv()

    def stage_b(p):
        for o in range(1, n_chip):
            there = ((c + n_chip - o) % n_chip) * CORES + r
            arrived(p, there)
            copy = remote(
                xk.at[place(p, there)], xk.at[place(p, there)], f_snd.at[o, p], k_rcv.at[p, there], seq=mate
            )
            copy.start()
            forward.append(copy)

    def stage_c(p):
        for o in range(n_chip):
            arrived(p, ((c + n_chip - o) % n_chip) * CORES + (1 - r))

        @pl.loop(0, tile // GROUP)
        def _(i):
            at = pl.ds(pl.multiple_of(i * GROUP, GROUP), GROUP)
            of = pl.ds(pl.multiple_of(p * tile + i * GROUP, GROUP), GROUP)
            xn[at, :] = (xk[of, :].astype(jnp.float32) * f_col[of, 0:1] * gain).astype(jnp.bfloat16)

        def product(chip):
            return jnp.dot(xn[...], wk[chip], preferred_element_type=jnp.float32)

        at = pl.ds(p * tile, tile)
        first, second = ends(p)
        psend[1, at, :] = product(n_chip - 1 - c).astype(jnp.bfloat16)
        sums(1, p, first).start()
        psend[0, at, :] = product(first).astype(jnp.bfloat16)
        sums(0, p, first).start()
        onward[at, :] = product(second)
        own[at, :] = product(c)

    def ends(p):
        beside, above = (c + 1 - 2 * (c % 2), (c + n_chip // 2) % n_chip)
        return (beside, above) if p % 2 == 0 else (above, beside)

    def sums(slot, p, chip):
        at = pl.ds(p * tile, tile)
        return remote(
            psend.at[slot, at], precv.at[slot, at], p_snd.at[slot, p], p_rcv.at[slot, p], seq=chip * CORES + r
        )

    def stage_d(p):
        _, second = ends(p)
        sums(1, p, second).wait_recv()

        @pl.loop(0, tile // GROUP)
        def _(i):
            at = pl.ds(pl.multiple_of(p * tile + i * GROUP, GROUP), GROUP)
            psend[2, at, :] = (onward[at, :] + precv[1, at, :].astype(jnp.float32)).astype(jnp.bfloat16)

        sums(2, p, second).start()

    for turn in range(PIECES + n_mp + 1):
        stage_a(turn)
        if turn == 0:
            factors()
        if turn == 1:
            spread_factors()
            for copy in local:
                copy.wait()
            for copy in w_out_copies:
                copy.wait()
        if 0 <= turn - n_mp < PIECES:
            stage_c(turn - n_mp)
        if 0 <= turn - (n_mp + 1) < PIECES:
            stage_d(turn - (n_mp + 1))
        if 0 <= turn - (n_mp - 1) < PIECES:
            stage_b(turn - (n_mp - 1))

    def gather_piece(p):
        for slot in (0, 2):
            sums(slot, p, c).wait_recv()

        @pl.loop(0, tile // GROUP)
        def _(i):
            at = pl.ds(pl.multiple_of(p * tile + i * GROUP, GROUP), GROUP)
            value = own[at, :]
            for slot in (0, 2):
                value = value + precv[slot, at, :].astype(jnp.float32)
            cand_n[at, :] = value[:, :LANES]
            gate_n[at, :] = value[:, LANES:] + bias

    for newton_step in range(NEWTON):
        zero = jnp.zeros((n_seq, LANES), jnp.float32)
        entering = zero if newton_step == 0 else carry[...]
        held = (entering, zero + 1.0, zero)
        for p in range(PIECES):
            if newton_step == 0:
                gather_piece(p)

            def lap(i, held):
                previous, a, b = held
                j = p * part + i
                at = pl.ds(p * tile + i, n_seq, stride=part)
                value, slope = cell(previous, cand_n[at, :], gate_n[at, :], rec_gate, rec_cand, 0.0)
                offset = value - slope * previous
                if newton_step > 0:
                    previous = sweep_a[j] * entering + sweep_b[j]
                a, b = (slope * a, slope * b + offset)
                sweep_a[j] = a
                sweep_b[j] = b
                return (previous, a, b)

            held = lax.fori_loop(0, part, lap, held, unroll=8)
        _, a, b = held
        state = jnp.zeros((1, LANES), jnp.float32)
        for i in range(n_seq):
            carry[i : i + 1, :] = state
            state = a[i : i + 1, :] * state + b[i : i + 1, :]
    entering = carry[...]
    for p in range(PIECES):

        @pl.loop(0, part, unroll=8)
        def _(i):
            j = p * part + i
            cand_n[pl.ds(p * tile + i, n_seq, stride=part), :] = sweep_a[j] * entering + sweep_b[j]

    for i in range(n_seq):
        for p in range(PIECES):
            start = (p * n_seq + i) * part
            ssend[i, p * part : (p + 1) * part, :] = cand_n[start : start + part, :].astype(jnp.bfloat16)
    lane = pl.ds(pl.multiple_of(q * LANES, LANES), LANES)
    spread = []
    for o in range(1, n_seq):
        there = (s + o) % n_seq
        copy = remote(ssend.at[there], sall.at[:, lane], s_snd.at[o], s_rcv.at[o], seq=there)
        copy.start()
        spread.append(copy)
    sall[:, lane] = ssend[pl.ds(s, 1)].reshape(rows, LANES)
    wo_copy.wait()
    for copy in spread:
        copy.wait_recv()

    cols = out_ref.shape[1]
    half = rows // HALVES

    def hop(side, d, h):
        there = (m + 1) % n_mp if side == 0 else (m + n_mp - 1) % n_mp
        at = pl.ds(h * half, half)
        return remote(
            osend.at[d, at], orecv.at[side, d, at], o_snd.at[d, h], o_rcv.at[side, d, h], mp=there
        )

    def project(d):
        lanes = pl.ds(pl.multiple_of(d * cols, cols), cols)
        pout[...] = jnp.dot(sall[...], wo[:, lanes], preferred_element_type=jnp.float32)

    for k in range(n_mp - 1, 0, -1):
        for side, sign in ((0, 1), (1, -1)):
            d = m + sign * k
            inside = (d <= n_mp - 1) if side == 0 else (d >= 0)
            first = (m == 0) if side == 0 else (m == n_mp - 1)

            @pl.when(inside)
            def _():
                project(d)
                for h in range(HALVES):
                    at = pl.ds(h * half, half)

                    @pl.when(first)
                    def _():
                        osend[d, at, :] = pout[at, :].astype(jnp.bfloat16)

                    @pl.when(jnp.logical_not(first))
                    def _():
                        hop(side, d, h).wait_recv()
                        osend[d, at, :] = (pout[at, :] + orecv[side, d, at, :].astype(jnp.float32)).astype(
                            jnp.bfloat16
                        )

                    hop(side, d, h).start()

    project(m)
    for side in range(2):

        @pl.when(m > 0 if side == 0 else m < n_mp - 1)
        def _():
            for h in range(HALVES):
                at = pl.ds(h * half, half)
                hop(side, m, h).wait_recv()
                pout[at, :] = pout[at, :] + orecv[side, m, at, :].astype(jnp.float32)

    out_ref[...] = pout[...].astype(jnp.bfloat16)

    for p in range(PIECES):
        for k in range(n_mp):
            for side, sign in ((0, -1), (1, 1)):
                b = m + sign * k

                @pl.when(not_last(side) & (b >= 0) & (b <= n_mp - 1))
                def _():
                    z_copy(side, tok_ref.at[piece(p)], b, p, k).wait_send()

            plane_copy(tok_ref.at[piece(p)], k, p).wait_send()
        for slot in range(3):
            sums(slot, p, c).wait_send()

    for copy in sq_copies + f_copies + forward + spread:
        copy.wait_send()
    for d in range(n_mp):

        @pl.when(d != m)
        def _():
            for h in range(HALVES):
                hop(0, d, h).wait_send()


def fused(n_seq, n_mp, tokens, norm_gain, w_cand, w_gate, rec_gate, rec_cand, bias_gate, w_out):
    rows, width = tokens.shape
    k_own, channels = w_cand.shape
    n_chip = n_seq // CORES
    length = rows * n_seq
    bf16, f32 = (jnp.bfloat16, jnp.float32)
    vmem, dma = (pltpu.VMEM, pltpu.SemaphoreType.DMA)
    whole = pl.BlockSpec(memory_space=pltpu.VMEM)
    far = pl.BlockSpec(memory_space=pl.ANY)
    per_channel = [part.reshape(n_seq, LANES) for part in (rec_gate, rec_cand, bias_gate)]
    return pl.pallas_call(
        functools.partial(fused_kernel, n_seq, n_mp),
        out_shape=jax.ShapeDtypeStruct((rows, width), bf16),
        in_specs=[whole, whole, far, far, whole, whole, whole, far],
        out_specs=whole,
        scratch_shapes=[
            vmem((n_mp, rows, width), bf16),
            vmem((length, width), bf16),
            vmem((length // PIECES, width), bf16),
            vmem((n_seq, LANES), f32),
            vmem((n_mp, n_seq, LANES), f32),
            vmem((n_seq, LANES), f32),
            vmem((n_seq, n_seq, LANES), f32),
            vmem((length, LANES), f32),
            vmem((n_chip, k_own * CORES, 2 * LANES), bf16),
            vmem(w_out.shape, bf16),
            vmem((length, 2 * LANES), f32),
            vmem((length, 2 * LANES), f32),
            vmem((n_chip - 1, length, 2 * LANES), bf16),
            vmem((n_chip - 1, length, 2 * LANES), bf16),
            vmem((length, LANES), f32),
            vmem((length, LANES), f32),
            vmem((rows, n_seq, LANES), f32),
            vmem((rows, n_seq, LANES), f32),
            vmem((n_seq, LANES), f32),
            vmem((n_seq, rows, LANES), bf16),
            vmem((rows, channels), bf16),
            vmem((rows, width), f32),
            vmem((n_mp, rows, width), bf16),
            vmem((2, n_mp, rows, width), bf16),
            dma((2, n_chip)),
            dma((2, n_chip)),
            dma((2, n_chip)),
            dma,
            dma((2, n_mp, PIECES)),
            dma((n_mp, PIECES)),
            dma((n_mp, PIECES)),
            dma((PIECES, n_seq)),
            dma((n_chip, PIECES)),
            dma((n_mp,)),
            dma((n_mp,)),
            dma((n_seq,)),
            dma((n_seq,)),
            dma((n_chip, PIECES)),
            dma((n_chip, PIECES)),
            dma((n_seq,)),
            dma((n_seq,)),
            dma((n_mp, HALVES)),
            dma((2, n_mp, HALVES)),
        ],
        compiler_params=pltpu.CompilerParams(collective_id=0, has_side_effects=True),
    )(tokens, norm_gain.reshape(n_mp, -1), w_cand, w_gate, *per_channel, w_out)


def layer(n_seq, n_mp, *args):
    tokens, w_cand = (args[0], args[2])
    fits = (
        n_seq == SUBLANES
        and n_seq == 4 * CORES
        and n_seq // CORES == n_mp
        and w_cand.shape[1] == n_seq * LANES
        and tokens.shape[0] == LANES
        and tokens.shape[1] % LANES == 0
    )
    return fused(n_seq, n_mp, *args) if fits else per_device(*args)


def solution(mesh):
    placed = (
        P("seq", "mp"),
        P(),
        P("seq", "mp"),
        P("seq", "mp"),
        P("mp"),
        P("mp"),
        P("mp"),
        P("mp", None),
    )
    return jax.shard_map(
        functools.partial(layer, mesh.shape["seq"], mesh.shape["mp"]), mesh=mesh, in_specs=placed, out_specs=P("seq", "mp"), check_vma=False
    )
```

```python
import functools

import jax
import jax.numpy as jnp
from jax import lax
from jax.experimental import pallas as pl
from jax.experimental.pallas import tpu as pltpu
from jax.sharding import PartitionSpec as P

NEWTON = 3


def prefix(value, axis, join, neutral):
    count, mine = (lax.axis_size(axis), lax.axis_index(axis))
    pieces = jax.tree.map(lambda part: lax.all_gather(part, axis), value)
    subtotal = jax.tree.map(
        lambda part, zero: jnp.full_like(part, 0) + jnp.asarray(zero, part.dtype), value, neutral
    )

    def lap(position, subtotal):
        longer = join(subtotal, jax.tree.map(lambda part: part[position], pieces))
        return jax.tree.map(lambda new, old: jnp.where(position < mine, new, old), longer, subtotal)

    return lax.fori_loop(0, count - 1, lap, subtotal)


def compose(earlier, later):
    return (later[0] * earlier[0], later[0] * earlier[1] + later[1])


def cell(previous, cand_pre, gate_pre, rec_gate, rec_cand, bias_gate):
    gate = jax.nn.sigmoid(gate_pre + rec_gate * previous + bias_gate)
    cand = jnp.tanh(cand_pre + rec_cand * previous)
    value = gate * previous + (1.0 - gate) * cand
    slope = (
        gate
        + gate * (1.0 - gate) * rec_gate * (previous - cand)
        + (1.0 - gate) * (1.0 - cand * cand) * rec_cand
    )
    return (value, slope)


def per_device(tokens, norm_gain, w_cand, w_gate, rec_gate, rec_cand, bias_gate, w_out):
    tok_rows = tokens.shape[0]
    channels = w_cand.shape[1]
    whole = lax.all_gather(tokens, "mp", axis=1, tiled=True)
    wide = whole.astype(jnp.float32)
    factor = lax.rsqrt(jnp.mean(wide * wide, axis=1, keepdims=True) + 1e-05)
    normed = (wide * factor * norm_gain).astype(jnp.bfloat16)
    cand_pre = jnp.dot(
        normed,
        lax.all_gather(w_cand, "seq", axis=0, tiled=True),
        preferred_element_type=jnp.float32,
    )
    gate_pre = jnp.dot(
        normed,
        lax.all_gather(w_gate, "seq", axis=0, tiled=True),
        preferred_element_type=jnp.float32,
    )
    state = jnp.zeros((tok_rows, channels), jnp.float32)
    carried = jnp.zeros((channels,), jnp.float32)
    ones_row = jnp.ones((channels,), jnp.float32)
    for newton_step in range(NEWTON):
        previous = jnp.concatenate([carried[None, :], state[:-1]], axis=0)
        value, slope = cell(previous, cand_pre, gate_pre, rec_gate, rec_cand, bias_gate)
        offset = value - slope * previous
        sweep_a, sweep_b = lax.associative_scan(compose, (slope, offset), axis=0)
        entering = prefix((sweep_a[-1], sweep_b[-1]), "seq", compose, (ones_row, carried * 0.0))
        carried = entering[1]
        state = sweep_a * carried + sweep_b
    state_b = state.astype(jnp.bfloat16)
    partial_sums = jnp.dot(state_b, w_out, preferred_element_type=jnp.float32)
    summed = lax.psum_scatter(partial_sums, "mp", scatter_dimension=1, tiled=True)
    return summed.astype(jnp.bfloat16)


CORES = 2
SUBLANES = 8
LANES = 128
PIECES = 8
HALVES = 2
GROUP = 16
MESH = pl.DeviceIdType.MESH


def fused_kernel(
    n_seq,
    n_mp,
    tok_ref,
    gain_ref,
    wc_hbm,
    wg_hbm,
    rg_ref,
    rc_ref,
    bg_ref,
    wo_hbm,
    out_ref,
    raw,
    xk,
    xn,
    sq_own,
    sq_all,
    f_own,
    f_all,
    f_col,
    wk,
    wo,
    own,
    onward,
    psend,
    precv,
    cand_n,
    gate_n,
    sweep_a,
    sweep_b,
    carry,
    ssend,
    sall,
    pout,
    osend,
    orecv,
    w_loc,
    w_snd,
    w_rcv,
    wo_sem,
    z_snd,
    z_rcv,
    k_snd,
    k_rcv,
    f_snd,
    q_snd,
    q_rcv,
    g_snd,
    g_rcv,
    p_snd,
    p_rcv,
    s_snd,
    s_rcv,
    o_snd,
    o_rcv,
):
    s, m = (lax.axis_index("seq"), lax.axis_index("mp"))
    n_chip = n_seq // CORES
    c, r = (s // CORES, s % CORES)
    mate = c * CORES + (1 - r)
    rows = tok_ref.shape[0]
    tokens = rows * n_seq
    k_own = wc_hbm.shape[0]
    width = raw.shape[2]
    q = r * n_chip + c

    def remote(src, dst, snd, rcv, **where):
        return pltpu.make_async_remote_copy(
            src_ref=src, dst_ref=dst, send_sem=snd, recv_sem=rcv, device_id=where, device_id_type=MESH
        )

    def barrier():
        sem = pltpu.get_barrier_semaphore()
        for o in range(1, n_seq):
            pl.semaphore_signal(sem, inc=1, device_id={"seq": (s + o) % n_seq}, device_id_type=MESH)
        for o in range(1, n_mp):
            pl.semaphore_signal(sem, inc=1, device_id={"mp": (m + o) % n_mp}, device_id_type=MESH)
        pl.semaphore_wait(sem, n_seq + n_mp - 2)

    def w_piece(hbm, core, chip):
        return hbm.at[:, pl.ds(pl.multiple_of((core * n_chip + chip) * LANES, LANES), LANES)]

    def w_place(i, chip, core):
        return wk.at[chip, pl.ds(pl.multiple_of(core * k_own, k_own), k_own), pl.ds(i * LANES, LANES)]

    local = [
        pltpu.make_async_copy(w_piece(hbm, r, chip), w_place(i, chip, r), w_loc.at[i, chip])
        for chip in range(n_chip)
        for i, hbm in enumerate((wc_hbm, wg_hbm))
    ]
    wo_copy = pltpu.make_async_copy(wo_hbm, wo, wo_sem)
    for copy in local:
        copy.start()
    barrier()

    part = rows // PIECES

    def piece(p):
        return pl.ds(p * part, part)

    def place(p, seq):
        return pl.ds(pl.multiple_of((p * n_seq + seq) * part, part), part)

    def z_copy(side, src, b, p, k):
        there = (m + 1) % n_mp if side == 0 else (m + n_mp - 1) % n_mp
        return remote(src, raw.at[b, piece(p)], z_snd.at[side, k, p], z_rcv.at[b, p], mp=there)

    def not_last(side):
        return m < n_mp - 1 if side == 0 else m > 0

    def plane_copy(src, b, p):
        seq = jnp.where(b == c, mate, b * CORES + r)
        return remote(src, xk.at[place(p, s)], k_snd.at[b, p], k_rcv.at[p, s], seq=seq)

    def send_own(p):
        mine = tok_ref.at[piece(p)]
        for side in range(2):

            @pl.when(not_last(side))
            def _():
                z_copy(side, mine, m, p, 0).start()

        plane_copy(mine, m, p).start()

        @pl.when(m == c)
        def _():
            xk[place(p, s), :] = tok_ref[piece(p), :]

    def pass_on(p, k):
        for side, sign in ((0, -1), (1, 1)):
            b = m + sign * k

            @pl.when((b >= 0) & (b <= n_mp - 1))
            def _():
                here = raw.at[b, piece(p)]
                z_copy(side, here, b, p, 0).wait_recv()

                @pl.when(not_last(side))
                def _():
                    z_copy(side, here, b, p, k).start()

                plane_copy(here, b, p).start()

                @pl.when(b == c)
                def _():
                    xk[place(p, s), :] = raw[b, piece(p), :]

    for p in range(min(2, PIECES)):
        send_own(p)

    across = lax.broadcasted_iota(jnp.int32, (rows, rows), 0) == lax.broadcasted_iota(
        jnp.int32, (rows, rows), 1
    )
    wide = tok_ref[...].astype(jnp.float32)
    squares = jnp.sum(wide * wide, axis=1, keepdims=True)
    squares = jnp.sum(jnp.where(across, squares, 0.0), axis=0, keepdims=True)
    sq_own[...] = jnp.broadcast_to(squares, sq_own.shape)
    sq_copies = []
    for o in range(1, n_mp):
        copy = remote(sq_own, sq_all.at[o], q_snd.at[o], q_rcv.at[o], mp=(m + o) % n_mp)
        copy.start()
        sq_copies.append(copy)

    w_out_copies = [
        remote(w_piece(hbm, 1 - r, chip), w_place(i, chip, r), w_snd.at[i, chip], w_rcv.at[i, chip], seq=mate)
        for chip in range(n_chip)
        for i, hbm in enumerate((wc_hbm, wg_hbm))
    ]
    for copy in w_out_copies:
        copy.start()
    wo_copy.start()
    gain = gain_ref[pl.ds(c, 1), :]
    bias = bg_ref[pl.ds(q, 1), :]
    rec_gate = rg_ref[pl.ds(q, 1), :]
    rec_cand = rc_ref[pl.ds(q, 1), :]
    tile = n_seq * part
    forward, f_copies = ([], [])

    def stage_a(turn):
        if turn + 2 < PIECES:
            send_own(turn + 2)
        for k in range(1, n_mp):
            p = turn - (k - 1)
            if 0 <= p < PIECES:
                pass_on(p, k)

    def factors():
        total = sq_own[...]
        for copy in sq_copies:
            copy.wait_recv()
        for o in range(1, n_mp):
            total = total + sq_all[o]
        f_own[...] = lax.rsqrt(total / (width * n_mp) + 1e-05)
        for o in range(1, n_seq):
            copy = remote(f_own, f_all.at[s], g_snd.at[o], g_rcv.at[s], seq=(s + o) % n_seq)
            copy.start()
            f_copies.append(copy)
        f_all[pl.ds(s, 1)] = f_own[...][None]

    def spread_factors():
        for o in range(1, n_seq):
            there = (s + o) % n_seq
            remote(f_own, f_all.at[there], g_snd.at[o], g_rcv.at[there], seq=there).wait_recv()
        for i in range(n_seq):
            row = f_all[i, 0:1, :]
            column = jnp.sum(jnp.where(across, row, 0.0), axis=1, keepdims=True)
            column = jnp.broadcast_to(column, (rows, LANES))
            for p in range(PIECES):
                f_col[(p * n_seq + i) * part : (p * n_seq + i + 1) * part, :] = column[
                    p * part : (p + 1) * part, :
                ]

    def arrived(p, seq):
        remote(tok_ref.at[piece(p)], xk.at[place(p, seq)], k_snd.at[0, p], k_rcv.at[p, seq], seq=mate).wait_recv()

    def stage_b(p):
        for o in range(1, n_chip):
            there = ((c + n_chip - o) % n_chip) * CORES + r
            arrived(p, there)
            copy = remote(
                xk.at[place(p, there)], xk.at[place(p, there)], f_snd.at[o, p], k_rcv.at[p, there], seq=mate
            )
            copy.start()
            forward.append(copy)

    def stage_c(p):
        for o in range(n_chip):
            arrived(p, ((c + n_chip - o) % n_chip) * CORES + (1 - r))

        @pl.loop(0, tile // GROUP)
        def _(i):
            at = pl.ds(pl.multiple_of(i * GROUP, GROUP), GROUP)
            of = pl.ds(pl.multiple_of(p * tile + i * GROUP, GROUP), GROUP)
            xn[at, :] = (xk[of, :].astype(jnp.float32) * f_col[of, 0:1] * gain).astype(jnp.bfloat16)

        def product(chip):
            return jnp.dot(xn[...], wk[chip], preferred_element_type=jnp.float32)

        at = pl.ds(p * tile, tile)
        first, second = ends(p)
        psend[1, at, :] = product(n_chip - 1 - c).astype(jnp.bfloat16)
        sums(1, p, first).start()
        psend[0, at, :] = product(first).astype(jnp.bfloat16)
        sums(0, p, first).start()
        onward[at, :] = product(second)
        own[at, :] = product(c)

    def ends(p):
        beside, above = (c + 1 - 2 * (c % 2), (c + n_chip // 2) % n_chip)
        return (beside, above) if p % 2 == 0 else (above, beside)

    def sums(slot, p, chip):
        at = pl.ds(p * tile, tile)
        return remote(
            psend.at[slot, at], precv.at[slot, at], p_snd.at[slot, p], p_rcv.at[slot, p], seq=chip * CORES + r
        )

    def stage_d(p):
        _, second = ends(p)
        sums(1, p, second).wait_recv()

        @pl.loop(0, tile // GROUP)
        def _(i):
            at = pl.ds(pl.multiple_of(p * tile + i * GROUP, GROUP), GROUP)
            psend[2, at, :] = (onward[at, :] + precv[1, at, :].astype(jnp.float32)).astype(jnp.bfloat16)

        sums(2, p, second).start()

    for turn in range(PIECES + n_mp + 1):
        stage_a(turn)
        if turn == 0:
            factors()
        if turn == 1:
            spread_factors()
            for copy in local:
                copy.wait()
            for copy in w_out_copies:
                copy.wait()
        if 0 <= turn - n_mp < PIECES:
            stage_c(turn - n_mp)
        if 0 <= turn - (n_mp - 1) < PIECES:
            stage_b(turn - (n_mp - 1))
        if 0 <= turn - (n_mp + 1) < PIECES:
            stage_d(turn - (n_mp + 1))

    def gather_piece(p):
        for slot in (0, 2):
            sums(slot, p, c).wait_recv()

        @pl.loop(0, tile // GROUP)
        def _(i):
            at = pl.ds(pl.multiple_of(p * tile + i * GROUP, GROUP), GROUP)
            value = own[at, :]
            for slot in (0, 2):
                value = value + precv[slot, at, :].astype(jnp.float32)
            cand_n[at, :] = value[:, :LANES]
            gate_n[at, :] = value[:, LANES:] + bias

    for newton_step in range(NEWTON):
        zero = jnp.zeros((n_seq, LANES), jnp.float32)
        entering = zero if newton_step == 0 else carry[...]
        held = (entering, zero + 1.0, zero)
        for p in range(PIECES):
            if newton_step == 0:
                gather_piece(p)

            def lap(i, held):
                previous, a, b = held
                j = p * part + i
                at = pl.ds(p * tile + i, n_seq, stride=part)
                value, slope = cell(previous, cand_n[at, :], gate_n[at, :], rec_gate, rec_cand, 0.0)
                offset = value - slope * previous
                if newton_step > 0:
                    previous = sweep_a[j] * entering + sweep_b[j]
                a, b = (slope * a, slope * b + offset)
                sweep_a[j] = a
                sweep_b[j] = b
                return (previous, a, b)

            held = lax.fori_loop(0, part, lap, held, unroll=8)
        _, a, b = held
        state = jnp.zeros((1, LANES), jnp.float32)
        for i in range(n_seq):
            carry[i : i + 1, :] = state
            state = a[i : i + 1, :] * state + b[i : i + 1, :]
    entering = carry[...]
    for p in range(PIECES):

        @pl.loop(0, part, unroll=8)
        def _(i):
            j = p * part + i
            cand_n[pl.ds(p * tile + i, n_seq, stride=part), :] = sweep_a[j] * entering + sweep_b[j]

    for i in range(n_seq):
        for p in range(PIECES):
            start = (p * n_seq + i) * part
            ssend[i, p * part : (p + 1) * part, :] = cand_n[start : start + part, :].astype(jnp.bfloat16)
    lane = pl.ds(pl.multiple_of(q * LANES, LANES), LANES)
    spread = []
    for o in range(1, n_seq):
        there = (s + o) % n_seq
        copy = remote(ssend.at[there], sall.at[:, lane], s_snd.at[o], s_rcv.at[o], seq=there)
        copy.start()
        spread.append(copy)
    sall[:, lane] = ssend[pl.ds(s, 1)].reshape(rows, LANES)
    wo_copy.wait()
    for copy in spread:
        copy.wait_recv()

    cols = out_ref.shape[1]
    half = rows // HALVES

    def hop(side, d, h):
        there = (m + 1) % n_mp if side == 0 else (m + n_mp - 1) % n_mp
        at = pl.ds(h * half, half)
        return remote(
            osend.at[d, at], orecv.at[side, d, at], o_snd.at[d, h], o_rcv.at[side, d, h], mp=there
        )

    def project(d):
        lanes = pl.ds(pl.multiple_of(d * cols, cols), cols)
        pout[...] = jnp.dot(sall[...], wo[:, lanes], preferred_element_type=jnp.float32)

    for k in range(n_mp - 1, 0, -1):
        for side, sign in ((0, 1), (1, -1)):
            d = m + sign * k
            inside = (d <= n_mp - 1) if side == 0 else (d >= 0)
            first = (m == 0) if side == 0 else (m == n_mp - 1)

            @pl.when(inside)
            def _():
                project(d)
                for h in range(HALVES):
                    at = pl.ds(h * half, half)

                    @pl.when(first)
                    def _():
                        osend[d, at, :] = pout[at, :].astype(jnp.bfloat16)

                    @pl.when(jnp.logical_not(first))
                    def _():
                        hop(side, d, h).wait_recv()
                        osend[d, at, :] = (pout[at, :] + orecv[side, d, at, :].astype(jnp.float32)).astype(
                            jnp.bfloat16
                        )

                    hop(side, d, h).start()

    project(m)
    for side in range(2):

        @pl.when(m > 0 if side == 0 else m < n_mp - 1)
        def _():
            for h in range(HALVES):
                at = pl.ds(h * half, half)
                hop(side, m, h).wait_recv()
                pout[at, :] = pout[at, :] + orecv[side, m, at, :].astype(jnp.float32)

    out_ref[...] = pout[...].astype(jnp.bfloat16)

    for p in range(PIECES):
        for k in range(n_mp):
            for side, sign in ((0, -1), (1, 1)):
                b = m + sign * k

                @pl.when(not_last(side) & (b >= 0) & (b <= n_mp - 1))
                def _():
                    z_copy(side, tok_ref.at[piece(p)], b, p, k).wait_send()

            plane_copy(tok_ref.at[piece(p)], k, p).wait_send()
        for slot in range(3):
            sums(slot, p, c).wait_send()

    for copy in sq_copies + f_copies + forward + spread:
        copy.wait_send()
    for d in range(n_mp):

        @pl.when(d != m)
        def _():
            for h in range(HALVES):
                hop(0, d, h).wait_send()


def fused(n_seq, n_mp, tokens, norm_gain, w_cand, w_gate, rec_gate, rec_cand, bias_gate, w_out):
    rows, width = tokens.shape
    k_own, channels = w_cand.shape
    n_chip = n_seq // CORES
    length = rows * n_seq
    bf16, f32 = (jnp.bfloat16, jnp.float32)
    vmem, dma = (pltpu.VMEM, pltpu.SemaphoreType.DMA)
    whole = pl.BlockSpec(memory_space=pltpu.VMEM)
    far = pl.BlockSpec(memory_space=pl.ANY)
    per_channel = [part.reshape(n_seq, LANES) for part in (rec_gate, rec_cand, bias_gate)]
    return pl.pallas_call(
        functools.partial(fused_kernel, n_seq, n_mp),
        out_shape=jax.ShapeDtypeStruct((rows, width), bf16),
        in_specs=[whole, whole, far, far, whole, whole, whole, far],
        out_specs=whole,
        scratch_shapes=[
            vmem((n_mp, rows, width), bf16),
            vmem((length, width), bf16),
            vmem((length // PIECES, width), bf16),
            vmem((n_seq, LANES), f32),
            vmem((n_mp, n_seq, LANES), f32),
            vmem((n_seq, LANES), f32),
            vmem((n_seq, n_seq, LANES), f32),
            vmem((length, LANES), f32),
            vmem((n_chip, k_own * CORES, 2 * LANES), bf16),
            vmem(w_out.shape, bf16),
            vmem((length, 2 * LANES), f32),
            vmem((length, 2 * LANES), f32),
            vmem((n_chip - 1, length, 2 * LANES), bf16),
            vmem((n_chip - 1, length, 2 * LANES), bf16),
            vmem((length, LANES), f32),
            vmem((length, LANES), f32),
            vmem((rows, n_seq, LANES), f32),
            vmem((rows, n_seq, LANES), f32),
            vmem((n_seq, LANES), f32),
            vmem((n_seq, rows, LANES), bf16),
            vmem((rows, channels), bf16),
            vmem((rows, width), f32),
            vmem((n_mp, rows, width), bf16),
            vmem((2, n_mp, rows, width), bf16),
            dma((2, n_chip)),
            dma((2, n_chip)),
            dma((2, n_chip)),
            dma,
            dma((2, n_mp, PIECES)),
            dma((n_mp, PIECES)),
            dma((n_mp, PIECES)),
            dma((PIECES, n_seq)),
            dma((n_chip, PIECES)),
            dma((n_mp,)),
            dma((n_mp,)),
            dma((n_seq,)),
            dma((n_seq,)),
            dma((n_chip, PIECES)),
            dma((n_chip, PIECES)),
            dma((n_seq,)),
            dma((n_seq,)),
            dma((n_mp, HALVES)),
            dma((2, n_mp, HALVES)),
        ],
        compiler_params=pltpu.CompilerParams(collective_id=0, has_side_effects=True),
    )(tokens, norm_gain.reshape(n_mp, -1), w_cand, w_gate, *per_channel, w_out)


def layer(n_seq, n_mp, *args):
    tokens, w_cand = (args[0], args[2])
    fits = (
        n_seq == SUBLANES
        and n_seq == 4 * CORES
        and n_seq // CORES == n_mp
        and w_cand.shape[1] == n_seq * LANES
        and tokens.shape[0] == LANES
        and tokens.shape[1] % LANES == 0
    )
    return fused(n_seq, n_mp, *args) if fits else per_device(*args)


def solution(mesh):
    placed = (
        P("seq", "mp"),
        P(),
        P("seq", "mp"),
        P("seq", "mp"),
        P("mp"),
        P("mp"),
        P("mp"),
        P("mp", None),
    )
    return jax.shard_map(
        functools.partial(layer, mesh.shape["seq"], mesh.shape["mp"]), mesh=mesh, in_specs=placed, out_specs=P("seq", "mp"), check_vma=False
    )
```
